512 devices in a mesh: seq: 32 (over x, y), dp: 8 (over z), domain: 2 (over core).
Axes of the slice: x: 4, y: 8, z: 8, core: 2. Of those that a mesh axis runs over, the one named last changes fastest.
Arguments:
- history: bfloat16 [2, 8, 8192, 1024], P('domain', 'dp', 'seq'), may hold values from -6 to 6
- qkv_weight: bfloat16 [2, 1024, 3072], P('domain', 'seq'), may hold values from -0.375 to 0.375
- norm_gain: float32 [2, 1024], P('domain'), may hold values from 0.1 to 1.9
- pool_gain: float32 [2, 1024], P('domain'), may hold values from 0.1 to 1.9
- lengths: int32 [2, 8], P('domain', 'dp'), may hold values from 1024 to 8192, as said below
- positives: int32 [8], replicated, may hold values from 0 to 7, each once
Outputs:
- user_vec: bfloat16 [2, 8, 1024], P('domain', 'dp', 'seq')
- loss: float32 [2, 8], P('domain', 'dp')
The draws below stay inside these ranges and needn't reach their ends.
Inputs may be any that keep to these rules, and one draw needn't show every extreme that they name: `lengths`: in each domain one user has exactly 8192 valid events and another exactly 1024. `positives`: each user of the second domain is named exactly once.
All inputs are finite; a program needn't handle non-finite values.
Results may differ from the reference program's by a relative error of at most 0.0085.
Values may be sent and summed in bfloat16 or wider, within the bound.
A program may use at most 64 MiB of HBM per device.

```python
import jax
import jax.numpy as jnp
from jax import lax

HEADS = 8
HEAD_DIM = 128
D = 1024
TOK_DEV = 256
LEN = 8192
USERS = 8


def draw_lengths(key, part):
    key_base, key_first, key_second = jax.random.split(key, 3)
    drawn = jax.random.randint(key_base, (2, USERS), LEN // 8, LEN + 1)
    longest = jax.random.randint(key_first, (2, 1), 0, USERS)
    shortest = (longest + 1 + jax.random.randint(key_second, (2, 1), 0, USERS - 1)) % USERS
    column = jnp.arange(USERS)[None, :]
    drawn = jnp.where(column == longest, LEN, drawn)
    drawn = jnp.where(column == shortest, LEN // 8, drawn)
    return drawn.astype(jnp.int32)


def draw_history(key, part):
    key_coef, key_pick, key_load, key_noise, key_level = jax.random.split(jax.random.fold_in(key, 7), 5)
    directions = 16
    block_count = LEN // TOK_DEV
    pair_count = TOK_DEV // 2
    leading = (2, USERS, block_count)
    coefficient = jax.random.normal(key_coef, leading + (pair_count, directions), jnp.float32)
    loading = jax.random.normal(key_load, leading + (1, D), jnp.float32)
    fresh_noise = jax.random.normal(key_noise, leading + (pair_count, 2, D), jnp.float32)
    noise_level = 0.6 + 0.0 * jax.random.uniform(key_level, leading + (1, 1, 1), jnp.float32)
    chosen = jax.random.randint(key_pick, leading + (1, D), 0, directions)
    chosen = jnp.broadcast_to(chosen, leading + (pair_count, D))
    picked = jnp.take_along_axis(coefficient, chosen, axis=-1)
    shared = picked * loading
    pair_sign = jnp.array([1.0, -1.0], jnp.float32)
    events = shared[..., None, :] * pair_sign[:, None] + noise_level * fresh_noise
    events = jnp.clip(events, -6.0, 6.0)
    return events.reshape(2, USERS, LEN, D).astype(jnp.bfloat16)


def level_of(stream_key, dims, cuts, smallest, largest):
    loudness = 1.0
    for axis_at, parts in cuts:
        draws = jax.random.uniform(jax.random.fold_in(jax.random.fold_in(stream_key, 6), axis_at), (parts,), jnp.float32, smallest / len(cuts), largest / len(cuts))
        loudness = loudness * jnp.repeat(jnp.exp(draws), dims[axis_at] // parts).reshape((-1,) + (1,) * (len(dims) - 1 - axis_at))
    return loudness


def gaussian(own_key, extent, spread, limit, cuts=(), dtype=jnp.bfloat16):
    factor_of = level_of(own_key, extent, cuts, -0.22, 0.18) if cuts else 1.0
    values = jax.random.normal(own_key, extent, jnp.float32) * spread * factor_of
    return jnp.minimum(jnp.maximum(values, -limit), limit).astype(dtype)


def setup_inputs(seed: int = 0) -> dict:
    streams_of = jax.random.split(jax.random.key(seed), 7)
    return {
        "history": draw_history(jax.random.fold_in(streams_of[6], 71), 0),
        "qkv_weight": gaussian(streams_of[1], (2, D, 3 * D), (D // 4) ** -0.5, 0.375, ((0, 2), (1, 32))),
        "norm_gain": jnp.clip(1.0 + 0.18 * jax.random.normal(streams_of[2], (2, D), jnp.float32), 0.1, 1.9),
        "pool_gain": jnp.clip(1.0 + 0.18 * jax.random.normal(streams_of[3], (2, D), jnp.float32), 0.1, 1.9),
        "lengths": draw_lengths(jax.random.fold_in(streams_of[6], 71), 0),
        "positives": jax.random.permutation(streams_of[5], USERS).astype(jnp.int32),
    }


logit_scale = 20.0
epsilon = 1e-06
highest = lax.Precision.HIGHEST

def feature_map(values):
    return jax.nn.elu(values) + 1.0

def attend_block(carry, block):
    state, total = carry
    queries, key_feats, val_feats = block
    queries_f = queries.astype(jnp.float32)
    keys_f = key_feats.astype(jnp.float32)
    values_f = val_feats.astype(jnp.float32)
    causal = jnp.arange(TOK_DEV)[:, None] >= jnp.arange(TOK_DEV)[None, :]
    scores = jnp.einsum('thc,shc->hts', queries_f, keys_f)
    scores = jnp.where(causal[None], scores, 0.0)
    denominator = lax.optimization_barrier(jnp.sum(scores, axis=-1)) + jnp.einsum('thc,hc->ht', queries_f, total, precision=highest)
    rounded = lax.optimization_barrier(scores.astype(jnp.bfloat16)).astype(jnp.float32)
    state_low = lax.optimization_barrier(state.astype(jnp.bfloat16)).astype(jnp.float32)
    numerator = jnp.einsum('hts,shc->thc', rounded, values_f) + jnp.einsum('thc,hcd->thd', queries_f, state_low)
    attended = numerator / jnp.transpose(denominator)[:, :, None]
    state = state + jnp.einsum('shc,shd->hcd', keys_f, values_f)
    total = total + lax.optimization_barrier(jnp.sum(keys_f, axis=0))
    return ((state, total), attended)

def tower(history_dom, weight, norm_row, pool_row, lengths_dom):

    def one_user(pair):
        events, length = pair
        wide = events.astype(jnp.float32)
        normed = (wide * lax.rsqrt(lax.optimization_barrier(jnp.mean(wide * wide, -1, keepdims=True)) + epsilon) * norm_row).astype(jnp.bfloat16)
        projected = jnp.dot(normed, weight, preferred_element_type=jnp.float32)
        valid = jnp.arange(LEN) < length
        queries = feature_map(projected[:, :D]).astype(jnp.bfloat16)
        key_feats = jnp.where(valid[:, None], feature_map(projected[:, D:2 * D]), 0.0).astype(jnp.bfloat16)
        val_feats = projected[:, 2 * D:].astype(jnp.bfloat16)
        shape = (LEN // TOK_DEV, TOK_DEV, HEADS, HEAD_DIM)
        start = (jnp.zeros((HEADS, HEAD_DIM, HEAD_DIM), jnp.float32), jnp.zeros((HEADS, HEAD_DIM), jnp.float32))
        final_state, attended = lax.scan(attend_block, start, (queries.reshape(shape), key_feats.reshape(shape), val_feats.reshape(shape)))
        attended = attended.reshape(LEN, D)
        return lax.optimization_barrier(jnp.sum(jnp.where(valid[:, None], wide + attended, 0.0), axis=0))
    pooled = lax.map(one_user, (history_dom, lengths_dom))
    factor = lax.rsqrt(lax.optimization_barrier(jnp.mean(pooled * pooled, -1, keepdims=True)) + epsilon)
    return (pooled * factor * pool_row).astype(jnp.bfloat16)

def reference(history, qkv_weight, norm_gain, pool_gain, lengths, positives):
    first = tower(history[0], qkv_weight[0], norm_gain[0], pool_gain[0], lengths[0])
    second = tower(history[1], qkv_weight[1], norm_gain[1], pool_gain[1], lengths[1])
    user_vec = jnp.stack([first, second])
    logits = jnp.dot(first, second.T, preferred_element_type=jnp.float32) * (logit_scale / D)
    pairing = positives[:, None] == jnp.arange(USERS)[None, :]
    chosen = jnp.where(pairing, logits, 0.0)
    loss_first = jnp.log(lax.optimization_barrier(jnp.sum(jnp.exp(logits), axis=1))) - lax.optimization_barrier(jnp.sum(chosen, axis=1))
    loss_second = jnp.log(lax.optimization_barrier(jnp.sum(jnp.exp(logits), axis=0))) - lax.optimization_barrier(jnp.sum(chosen, axis=0))
    return (user_vec, jnp.stack([loss_first, loss_second]))
```

```python
import jax
import jax.numpy as jnp
from jax import lax
from jax.experimental import pallas as pl
from jax.experimental.pallas import tpu as pltpu
from jax.sharding import PartitionSpec as P

HEAD_DIM = 128
NX = 4
NY = 8
NZ = 8
TOK = 256
HALF = 128
WIDTH = 1024
ROWS = 32

logit_scale = 20.0
epsilon = 1e-06
f32 = jnp.float32
bf16 = jnp.bfloat16
MESH = pl.DeviceIdType.MESH


def phi(a):
    return jnp.where(a > 0.0, a + 1.0, jnp.exp(jnp.minimum(a, 0.0)))


def tower_kernel(
    lengths_ref,
    positives_ref,
    hist_ref,
    wt_ref,
    gain_ref,
    pool_gain_ref,
    vec_ref,
    loss_ref,
    tok,
    w_all,
    q_all,
    nd_all,
    st_all,
    sx,
    px,
    py,
    vz,
    uz,
    local_sem,
    wy_send,
    wy_recv,
    wx_send,
    wx_recv,
    r_send,
    r_recv,
    l_send,
    l_recv,
    s_send,
    s_recv,
    px_send,
    px_recv,
    py_send,
    py_recv,
    uz_send,
    uz_recv,
):
    seq = lax.axis_index("seq")
    z = lax.axis_index("dp")
    core = lax.axis_index("domain")
    x = seq // NY
    y = lax.rem(seq, NY)
    length = lengths_ref[0, 0]

    def y_peer(k):
        return {"seq": x * NY + lax.rem(y + k, NY)}

    def x_peer(k):
        return {"seq": lax.rem(x + k, NX) * NY + y}

    def z_peer(k):
        return {"dp": lax.rem(z + k, NZ), "domain": 1 - core}

    def remote(src, dst, send, recv, device):
        return pltpu.make_async_remote_copy(
            src_ref=src, dst_ref=dst, send_sem=send, recv_sem=recv,
            device_id=device, device_id_type=MESH,
        )

    barrier = pltpu.get_barrier_semaphore()
    for k in range(1, NY):
        pl.semaphore_signal(barrier, inc=1, device_id=y_peer(k), device_id_type=MESH)
    for k in range(1, NX):
        pl.semaphore_signal(barrier, inc=1, device_id=x_peer(k), device_id_type=MESH)
    for k in range(NZ):
        pl.semaphore_signal(barrier, inc=1, device_id=z_peer(k), device_id_type=MESH)
    pl.semaphore_wait(barrier, NY - 1 + NX - 1 + NZ)

    def wy_slot(owner):
        return w_all.at[x, pl.ds(pl.multiple_of(owner * ROWS, ROWS), ROWS)]

    wy = []
    for k in range(1, NY):
        to = lax.rem(y + k, NY)
        c = remote(wt_ref.at[to], wy_slot(y), wy_send.at[k], wy_recv.at[k], y_peer(k))
        c.start()
        wy.append(c)
    own = pltpu.make_async_copy(wt_ref.at[y], wy_slot(y), local_sem)
    own.start()

    def stream(i, right, receiving):
        hop = i // 2 + (1 if receiving else 0)
        half = i % 2 if right else 1 - i % 2
        slot = lax.rem(y + (NY - hop if right else hop), NY)
        rows = pl.ds(half * HALF, HALF)
        dst = tok.at[slot, rows]
        src = hist_ref.at[rows] if hop == 0 else dst
        send, recv = (r_send, r_recv) if right else (l_send, l_recv)
        return remote(src, dst, send.at[i], recv.at[i], y_peer(1 if right else NY - 1))

    sent = []

    def send(i):
        for right in (True, False):
            c = stream(i, right, False)
            c.start()
            sent.append(c)

    def arrive(i):
        for right in (True, False):
            stream(i, right, True).wait_recv()
            if i + 2 <= 6:
                c = stream(i + 2, right, False)
                c.start()
                sent.append(c)

    send(0)
    send(1)

    for k in range(1, NY):
        slot = wy_slot(lax.rem(y + NY - k, NY))
        remote(slot, slot, wy_send.at[k], wy_recv.at[k], y_peer(k)).wait_recv()
    own.wait()
    wx = []
    for k in range(1, NX):
        c = remote(w_all.at[x], w_all.at[x], wx_send.at[k], wx_recv.at[k], x_peer(k))
        c.start()
        wx.append(c)

    gain = gain_ref[...]
    ones = jnp.ones((TOK, HEAD_DIM), bf16)
    row = lax.broadcasted_iota(jnp.int32, (TOK, 1), 0)
    causal = lax.broadcasted_iota(jnp.int32, (TOK, TOK), 0) >= lax.broadcasted_iota(
        jnp.int32, (TOK, TOK), 1
    )
    head_cols = pl.ds(pl.multiple_of(y * HEAD_DIM, HEAD_DIM), HEAD_DIM)

    def compute(src, slot, pooled):
        valid = (x * NY + slot) * TOK + row < length
        wide = src[...].astype(f32)
        scale = lax.rsqrt(jnp.sum(wide * wide, -1, keepdims=True) * (1.0 / WIDTH) + epsilon)
        normed = (wide * scale * gain).astype(bf16)
        weight = w_all[...].reshape(WIDTH, 3 * HEAD_DIM)
        proj = jnp.dot(normed, weight, preferred_element_type=f32)
        q = phi(proj[:, :HEAD_DIM]).astype(bf16)
        k = jnp.where(valid, phi(proj[:, HEAD_DIM : 2 * HEAD_DIM]), 0.0).astype(bf16)
        v1 = jnp.concatenate([proj[:, 2 * HEAD_DIM :].astype(bf16), ones], axis=1)
        scores = lax.dot_general(q, k, (((1,), (1,)), ((), ())), preferred_element_type=f32)
        low = jnp.where(causal, scores, 0.0).astype(bf16)
        q_all[slot] = q
        nd_all[slot] = jnp.dot(low, v1, preferred_element_type=f32)
        st_all[slot] = lax.dot_general(
            k, v1, (((0,), (0,)), ((), ())), preferred_element_type=f32
        )
        mine = src[:, head_cols].astype(f32)
        return pooled + jnp.sum(jnp.where(valid, mine, 0.0), axis=0, keepdims=True)

    def block(hop, pooled):
        slot = lax.rem(y + NY + hop, NY)
        return compute(tok.at[slot], slot, pooled)

    pooled = jnp.zeros((1, HEAD_DIM), f32)
    arrive(0)
    for k in range(1, NX):
        slot = w_all.at[lax.rem(x + NX - k, NX)]
        remote(slot, slot, wx_send.at[k], wx_recv.at[k], x_peer(k)).wait_recv()
    pooled = compute(hist_ref, y, pooled)
    arrive(1)
    pooled = block(-1, pooled)
    arrive(2)
    pooled = block(1, pooled)
    arrive(3)
    pooled = block(-2, pooled)
    arrive(4)
    pooled = block(2, pooled)
    arrive(5)
    pooled = block(-3, pooled)
    pooled = block(3, pooled)
    arrive(6)
    pooled = block(4, pooled)

    total = st_all[0]
    for b in range(1, NY):
        total = total + st_all[b]
    sx[x] = total.astype(bf16)
    ss = []
    for k in range(1, NX):
        c = remote(sx.at[x], sx.at[x], s_send.at[k], s_recv.at[k], x_peer(k))
        c.start()
        ss.append(c)
    run = st_all[0]
    for b in range(1, NY):
        nd_all[b] = nd_all[b] + jnp.dot(q_all[b], run.astype(bf16), preferred_element_type=f32)
        if b + 1 < NY:
            run = run + st_all[b]
    for k in range(1, NX):
        slot = sx.at[lax.rem(x + NX - k, NX)]
        remote(slot, slot, s_send.at[k], s_recv.at[k], x_peer(k)).wait_recv()
    before = jnp.zeros((HEAD_DIM, 2 * HEAD_DIM), f32)
    for g in range(NX - 1):
        before = before + jnp.where(g < x, sx[g].astype(f32), 0.0)
    before = before.astype(bf16)
    for b in range(NY):
        nd = nd_all[b] + jnp.dot(q_all[b], before, preferred_element_type=f32)
        valid = (x * NY + b) * TOK + row < length
        attended = nd[:, :HEAD_DIM] / nd[:, HEAD_DIM:]
        pooled = pooled + jnp.sum(jnp.where(valid, attended, 0.0), axis=0, keepdims=True)

    px[x] = jnp.broadcast_to(pooled, (8, HEAD_DIM))
    ps = []
    for k in range(1, NX):
        c = remote(px.at[x], px.at[x], px_send.at[k], px_recv.at[k], x_peer(k))
        c.start()
        ps.append(c)
    for k in range(1, NX):
        slot = px.at[lax.rem(x + NX - k, NX)]
        remote(slot, slot, px_send.at[k], px_recv.at[k], x_peer(k)).wait_recv()
    py[y] = px[0] + px[1] + px[2] + px[3]
    for k in range(1, NY):
        c = remote(py.at[y], py.at[y], py_send.at[k], py_recv.at[k], y_peer(k))
        c.start()
        ps.append(c)
    for k in range(1, NY):
        slot = py.at[lax.rem(y + NY - k, NY)]
        remote(slot, slot, py_send.at[k], py_recv.at[k], y_peer(k)).wait_recv()
    head_row = lax.broadcasted_iota(jnp.int32, (8, HEAD_DIM), 0)
    full = jnp.zeros((8, HEAD_DIM), f32)
    for h in range(NY):
        full = jnp.where(head_row == h, py[h], full)
    square = jnp.sum(jnp.sum(full * full, axis=1, keepdims=True), axis=0, keepdims=True)
    factor = lax.rsqrt(square * (1.0 / WIDTH) + epsilon)
    vec = (full * factor * pool_gain_ref[...]).astype(bf16).astype(f32)
    vec_ref[...] = vec
    vz[...] = vec

    for k in range(NZ):
        c = remote(vz, uz.at[z], uz_send.at[k], uz_recv.at[k], z_peer(k))
        c.start()
        ps.append(c)
    for k in range(NZ):
        slot = uz.at[lax.rem(z + NZ - k, NZ)]
        remote(vz, slot, uz_send.at[k], uz_recv.at[k], z_peer(k)).wait_recv()
    logits = jnp.sum(jnp.sum(uz[...] * vec[None], axis=1), axis=-1, keepdims=True)
    logits = logits * (logit_scale / WIDTH)
    user = lax.broadcasted_iota(jnp.int32, (8, 1), 0)
    names = jnp.zeros((8, 1), jnp.int32)
    target = jnp.int32(0)
    for j in range(NZ):
        names = jnp.where(user == j, positives_ref[0, j], names)
        target = jnp.where(z == j, positives_ref[0, j], target)
    partner = jnp.where(core == 0, (user == target).astype(f32), (names == z).astype(f32))
    loss = jnp.log(jnp.sum(jnp.exp(logits), axis=0, keepdims=True)) - jnp.sum(
        jnp.where(partner > 0.5, logits, 0.0), axis=0, keepdims=True
    )
    loss_ref[...] = jnp.broadcast_to(loss, (8, HEAD_DIM))

    for c in wy + wx + sent + ss + ps:
        c.wait_send()


def shards(history, qkv_weight, norm_gain, pool_gain, lengths, positives):
    seq_place = lax.axis_index("seq")
    wt = qkv_weight[0].reshape(ROWS, 3, NY, HEAD_DIM).transpose(2, 0, 1, 3)
    wt = wt.reshape(NY, ROWS, 3 * HEAD_DIM)
    dma = pltpu.SemaphoreType.DMA
    vmem = pl.BlockSpec(memory_space=pltpu.VMEM)
    smem = pl.BlockSpec(memory_space=pltpu.SMEM)
    vec, loss = pl.pallas_call(
        tower_kernel,
        out_shape=(
            jax.ShapeDtypeStruct((8, HEAD_DIM), f32),
            jax.ShapeDtypeStruct((8, HEAD_DIM), f32),
        ),
        in_specs=[smem, smem, vmem, vmem, vmem, vmem],
        out_specs=(vmem, vmem),
        scratch_shapes=[
            pltpu.VMEM((NY, TOK, WIDTH), bf16),
            pltpu.VMEM((NX, NY * ROWS, 3 * HEAD_DIM), bf16),
            pltpu.VMEM((NY, TOK, HEAD_DIM), bf16),
            pltpu.VMEM((NY, TOK, 2 * HEAD_DIM), f32),
            pltpu.VMEM((NY, HEAD_DIM, 2 * HEAD_DIM), f32),
            pltpu.VMEM((NX, HEAD_DIM, 2 * HEAD_DIM), bf16),
            pltpu.VMEM((NX, 8, HEAD_DIM), f32),
            pltpu.VMEM((NY, 8, HEAD_DIM), f32),
            pltpu.VMEM((8, HEAD_DIM), f32),
            pltpu.VMEM((NZ, 8, HEAD_DIM), f32),
            dma,
            dma((NY,)),
            dma((NY,)),
            dma((NX,)),
            dma((NX,)),
            dma((7,)),
            dma((7,)),
            dma((7,)),
            dma((7,)),
            dma((NX,)),
            dma((NX,)),
            dma((NX,)),
            dma((NX,)),
            dma((NY,)),
            dma((NY,)),
            dma((NZ,)),
            dma((NZ,)),
        ],
        compiler_params=pltpu.CompilerParams(collective_id=0, has_side_effects=True),
    )(
        lengths,
        positives.reshape(1, NZ),
        history[0, 0],
        wt,
        norm_gain,
        pool_gain.reshape(8, HEAD_DIM),
    )
    out = lax.dynamic_slice_in_dim(vec.reshape(1, 1, WIDTH), seq_place * ROWS, ROWS, 2)
    return out.astype(bf16), loss[:1, :1]


def solution(mesh):
    placed = (
        P("domain", "dp", "seq", None),
        P("domain", "seq", None),
        P("domain", None),
        P("domain", None),
        P("domain", "dp"),
        P(),
    )
    return jax.shard_map(
        shards,
        mesh=mesh,
        in_specs=placed,
        out_specs=(P("domain", "dp", "seq"), P("domain", "dp")),
        check_vma=False,
    )
```

```python
import jax
import jax.numpy as jnp
from jax import lax
from jax.experimental import pallas as pl
from jax.experimental.pallas import tpu as pltpu
from jax.sharding import PartitionSpec as P

HEAD_DIM = 128
NX = 4
NY = 8
NZ = 8
TOK = 256
HALF = 128
WIDTH = 1024
ROWS = 32

logit_scale = 20.0
epsilon = 1e-06
f32 = jnp.float32
bf16 = jnp.bfloat16
MESH = pl.DeviceIdType.MESH


def phi(a):
    return jnp.where(a > 0.0, a + 1.0, jnp.exp(jnp.minimum(a, 0.0)))


def tower_kernel(
    lengths_any,
    positives_any,
    hist_any,
    qkv_any,
    gain_any,
    pool_gain_any,
    vec_ref,
    loss_ref,
    lengths_ref,
    positives_ref,
    gain_ref,
    pool_gain_ref,
    tok,
    w_all,
    q_all,
    nd_all,
    st_all,
    sx,
    px,
    py,
    vz,
    uz,
    local_sem,
    wl_sem,
    wy_send,
    wy_recv,
    wz_send,
    wz_recv,
    wx_send,
    wx_recv,
    r_send,
    r_recv,
    l_send,
    l_recv,
    s_send,
    s_recv,
    px_send,
    px_recv,
    py_send,
    py_recv,
    uz_send,
    uz_recv,
):
    seq = lax.axis_index("seq")
    z = lax.axis_index("dp")
    core = lax.axis_index("domain")
    x = seq // NY
    y = lax.rem(seq, NY)

    def y_peer(k):
        return {"seq": x * NY + lax.rem(y + k, NY)}

    def x_peer(k):
        return {"seq": lax.rem(x + k, NX) * NY + y}

    def z_peer(k):
        return {"dp": lax.rem(z + k, NZ), "domain": 1 - core}

    def w_peer(k):
        return {"dp": lax.rem(z + k, NZ)}

    def remote(src, dst, send, recv, device):
        return pltpu.make_async_remote_copy(
            src_ref=src, dst_ref=dst, send_sem=send, recv_sem=recv,
            device_id=device, device_id_type=MESH,
        )

    barrier = pltpu.get_barrier_semaphore()
    for k in range(1, NY):
        pl.semaphore_signal(barrier, inc=1, device_id=y_peer(k), device_id_type=MESH)
    for k in range(1, NX):
        pl.semaphore_signal(barrier, inc=1, device_id=x_peer(k), device_id_type=MESH)
    for k in range(NZ):
        pl.semaphore_signal(barrier, inc=1, device_id=z_peer(k), device_id_type=MESH)
    for k in range(1, NZ):
        pl.semaphore_signal(barrier, inc=1, device_id=w_peer(k), device_id_type=MESH)
    fetched = []
    for i, (src, dst) in enumerate(
        (
            (hist_any.at[0, 0], tok.at[y]),
            (lengths_any, lengths_ref),
            (positives_any, positives_ref),
            (gain_any, gain_ref),
            (pool_gain_any, pool_gain_ref),
        )
    ):
        c = pltpu.make_async_copy(src, dst, local_sem.at[i])
        c.start()
        fetched.append(c)
    pl.semaphore_wait(barrier, NY - 1 + NX - 1 + NZ + NZ - 1)
    fetched[0].wait()

    def w_slot(owner):
        return w_all.at[x, pl.ds(pl.multiple_of(owner * ROWS, ROWS), ROWS)]

    def w_part(i):
        rows = pl.ds(pl.multiple_of(z * ROWS, ROWS), ROWS)
        return w_all.at[x, rows, pl.ds(i * HEAD_DIM, HEAD_DIM)]

    def w_columns(i, head):
        start = pl.multiple_of(i * WIDTH + head * HEAD_DIM, HEAD_DIM)
        return qkv_any.at[0, :, pl.ds(start, HEAD_DIM)]

    def w_to_y(k, i):
        src = w_columns(i, lax.rem(y + k, NY))
        return remote(src, w_part(i), wy_send.at[k, i], wy_recv.at[i], y_peer(k))

    def w_own(i):
        return pltpu.make_async_copy(w_columns(i, y), w_part(i), wl_sem.at[i])

    @pl.when(y == z)
    def _():
        for i in range(3):
            w_own(i).start()
        for k in range(1, NY):
            for i in range(3):
                w_to_y(k, i).start()

    def stream(i, right, receiving):
        hop = i // 2 + (1 if receiving else 0)
        half = i % 2 if right else 1 - i % 2
        slot = lax.rem(y + (NY - hop if right else hop), NY)
        rows = pl.ds(half * HALF, HALF)
        dst = tok.at[slot, rows]
        send, recv = (r_send, r_recv) if right else (l_send, l_recv)
        return remote(dst, dst, send.at[i], recv.at[i], y_peer(1 if right else NY - 1))

    sent = []

    def send(i):
        for right in (True, False):
            c = stream(i, right, False)
            c.start()
            sent.append(c)

    def arrive(i):
        for right in (True, False):
            stream(i, right, True).wait_recv()
            if i + 2 <= 6:
                c = stream(i + 2, right, False)
                c.start()
                sent.append(c)

    send(0)
    send(1)

    @pl.when(y == z)
    def _():
        for i in range(3):
            w_own(i).wait()

    @pl.when(y != z)
    def _():
        for i in range(3):
            remote(w_part(i), w_part(i), wy_send.at[0, i], wy_recv.at[i], y_peer(1)).wait_recv()

    wz = []
    for k in range(1, NZ):
        c = remote(w_slot(z), w_slot(z), wz_send.at[k], wz_recv.at[k], w_peer(k))
        c.start()
        wz.append(c)
    for c in fetched[1:]:
        c.wait()
    length = lengths_ref[0, 0]
    for k in range(1, NZ):
        slot = w_slot(lax.rem(z + NZ - k, NZ))
        remote(slot, slot, wz_send.at[k], wz_recv.at[k], w_peer(k)).wait_recv()
    wx = []
    for k in range(1, NX):
        c = remote(w_all.at[x], w_all.at[x], wx_send.at[k], wx_recv.at[k], x_peer(k))
        c.start()
        wx.append(c)

    gain = gain_ref[...]
    ones = jnp.ones((TOK, HEAD_DIM), bf16)
    row = lax.broadcasted_iota(jnp.int32, (TOK, 1), 0)
    causal = lax.broadcasted_iota(jnp.int32, (TOK, TOK), 0) >= lax.broadcasted_iota(
        jnp.int32, (TOK, TOK), 1
    )
    head_cols = pl.ds(pl.multiple_of(y * HEAD_DIM, HEAD_DIM), HEAD_DIM)

    def compute(src, slot, pooled):
        valid = (x * NY + slot) * TOK + row < length
        wide = src[...].astype(f32)
        scale = lax.rsqrt(jnp.sum(wide * wide, -1, keepdims=True) * (1.0 / WIDTH) + epsilon)
        normed = (wide * scale * gain).astype(bf16)
        weight = w_all[...].reshape(WIDTH, 3 * HEAD_DIM)
        proj = jnp.dot(normed, weight, preferred_element_type=f32)
        q = phi(proj[:, :HEAD_DIM]).astype(bf16)
        k = jnp.where(valid, phi(proj[:, HEAD_DIM : 2 * HEAD_DIM]), 0.0).astype(bf16)
        v1 = jnp.concatenate([proj[:, 2 * HEAD_DIM :].astype(bf16), ones], axis=1)
        scores = lax.dot_general(q, k, (((1,), (1,)), ((), ())), preferred_element_type=f32)
        low = jnp.where(causal, scores, 0.0).astype(bf16)
        q_all[slot] = q
        nd_all[slot] = jnp.dot(low, v1, preferred_element_type=f32)
        st_all[slot] = lax.dot_general(
            k, v1, (((0,), (0,)), ((), ())), preferred_element_type=f32
        )
        mine = src[:, head_cols].astype(f32)
        return pooled + jnp.sum(jnp.where(valid, mine, 0.0), axis=0, keepdims=True)

    def block(hop, pooled):
        slot = lax.rem(y + NY + hop, NY)
        return compute(tok.at[slot], slot, pooled)

    pooled = jnp.zeros((1, HEAD_DIM), f32)
    arrive(0)
    for k in range(1, NX):
        slot = w_all.at[lax.rem(x + NX - k, NX)]
        remote(slot, slot, wx_send.at[k], wx_recv.at[k], x_peer(k)).wait_recv()
    pooled = block(0, pooled)
    arrive(1)
    pooled = block(-1, pooled)
    arrive(2)
    pooled = block(1, pooled)
    arrive(3)
    pooled = block(-2, pooled)
    arrive(4)
    pooled = block(2, pooled)
    arrive(5)
    pooled = block(-3, pooled)
    pooled = block(3, pooled)
    arrive(6)
    pooled = block(4, pooled)

    total = st_all[0]
    for b in range(1, NY):
        total = total + st_all[b]
    total_rows = jnp.transpose(total[:, HEAD_DIM:])[:16]
    sx[x] = jnp.concatenate([total[:, :HEAD_DIM], total_rows], axis=0).astype(bf16)
    ss = []
    for k in range(1, NX):
        c = remote(sx.at[x], sx.at[x], s_send.at[k], s_recv.at[k], x_peer(k))
        c.start()
        ss.append(c)
    run = st_all[0]
    for b in range(1, NY):
        nd_all[b] = nd_all[b] + jnp.dot(q_all[b], run.astype(bf16), preferred_element_type=f32)
        if b + 1 < NY:
            run = run + st_all[b]
    for k in range(1, NX):
        slot = sx.at[lax.rem(x + NX - k, NX)]
        remote(slot, slot, s_send.at[k], s_recv.at[k], x_peer(k)).wait_recv()
    before = jnp.zeros((HEAD_DIM + 16, HEAD_DIM), f32)
    for g in range(NX - 1):
        before = before + jnp.where(g < x, sx[g].astype(f32), 0.0)
    total_before = jnp.broadcast_to(before[HEAD_DIM : HEAD_DIM + 1], (HEAD_DIM, HEAD_DIM))
    before = jnp.concatenate([before[:HEAD_DIM], jnp.transpose(total_before)], axis=1)
    before = before.astype(bf16)
    for b in range(NY):
        nd = nd_all[b] + jnp.dot(q_all[b], before, preferred_element_type=f32)
        valid = (x * NY + b) * TOK + row < length
        attended = nd[:, :HEAD_DIM] / nd[:, HEAD_DIM:]
        pooled = pooled + jnp.sum(jnp.where(valid, attended, 0.0), axis=0, keepdims=True)

    px[x] = jnp.broadcast_to(pooled, (8, HEAD_DIM))
    ps = []
    for k in range(1, NX):
        c = remote(px.at[x], px.at[x], px_send.at[k], px_recv.at[k], x_peer(k))
        c.start()
        ps.append(c)
    for k in range(1, NX):
        slot = px.at[lax.rem(x + NX - k, NX)]
        remote(slot, slot, px_send.at[k], px_recv.at[k], x_peer(k)).wait_recv()
    py[y] = px[0] + px[1] + px[2] + px[3]
    for k in range(1, NY):
        c = remote(py.at[y], py.at[y], py_send.at[k], py_recv.at[k], y_peer(k))
        c.start()
        ps.append(c)
    for k in range(1, NY):
        slot = py.at[lax.rem(y + NY - k, NY)]
        remote(slot, slot, py_send.at[k], py_recv.at[k], y_peer(k)).wait_recv()
    head_row = lax.broadcasted_iota(jnp.int32, (8, HEAD_DIM), 0)
    full = jnp.zeros((8, HEAD_DIM), f32)
    for h in range(NY):
        full = jnp.where(head_row == h, py[h], full)
    square = jnp.sum(jnp.sum(full * full, axis=1, keepdims=True), axis=0, keepdims=True)
    factor = lax.rsqrt(square * (1.0 / WIDTH) + epsilon)
    vec = (full * factor * pool_gain_ref[...]).astype(bf16).astype(f32)
    vz[...] = vec
    head_vec = jnp.sum(jnp.where(head_row == seq // 4, vec, 0.0), axis=0, keepdims=True)
    piece = jnp.zeros((1, ROWS), f32)
    for j in range(4):
        part = head_vec[:, j * ROWS : (j + 1) * ROWS]
        piece = jnp.where(lax.rem(seq, 4) == j, part, piece)
    vec_ref[...] = piece.astype(bf16)

    for k in range(NZ):
        c = remote(vz, uz.at[z], uz_send.at[k], uz_recv.at[k], z_peer(k))
        c.start()
        ps.append(c)
    for k in range(NZ):
        slot = uz.at[lax.rem(z + NZ - k, NZ)]
        remote(vz, slot, uz_send.at[k], uz_recv.at[k], z_peer(k)).wait_recv()
    logits = jnp.sum(jnp.sum(uz[...] * vec[None], axis=1), axis=-1, keepdims=True)
    logits = logits * (logit_scale / WIDTH)
    user = lax.broadcasted_iota(jnp.int32, (8, 1), 0)
    names = jnp.zeros((8, 1), jnp.int32)
    target = jnp.int32(0)
    for j in range(NZ):
        names = jnp.where(user == j, positives_ref[0, j], names)
        target = jnp.where(z == j, positives_ref[0, j], target)
    partner = jnp.where(core == 0, (user == target).astype(f32), (names == z).astype(f32))
    loss = jnp.log(jnp.sum(jnp.exp(logits), axis=0, keepdims=True)) - jnp.sum(
        jnp.where(partner > 0.5, logits, 0.0), axis=0, keepdims=True
    )
    loss_ref[...] = loss

    for c in wz + wx + sent + ss + ps:
        c.wait_send()

    @pl.when(y == z)
    def _():
        for k in range(1, NY):
            for i in range(3):
                w_to_y(k, i).wait_send()


def shards(history, qkv_weight, norm_gain, pool_gain, lengths, positives):
    dma = pltpu.SemaphoreType.DMA
    vmem = pl.BlockSpec(memory_space=pltpu.VMEM)
    hbm = pl.BlockSpec(memory_space=pltpu.HBM)
    vec, loss = pl.pallas_call(
        tower_kernel,
        out_shape=(
            jax.ShapeDtypeStruct((1, ROWS), bf16),
            jax.ShapeDtypeStruct((1, 1), f32),
        ),
        in_specs=[hbm] * 6,
        out_specs=(vmem, vmem),
        scratch_shapes=[
            pltpu.SMEM((1, 1), jnp.int32),
            pltpu.SMEM((1, NZ), jnp.int32),
            pltpu.VMEM((1, WIDTH), f32),
            pltpu.VMEM((8, HEAD_DIM), f32),
            pltpu.VMEM((NY, TOK, WIDTH), bf16),
            pltpu.VMEM((NX, NY * ROWS, 3 * HEAD_DIM), bf16),
            pltpu.VMEM((NY, TOK, HEAD_DIM), bf16),
            pltpu.VMEM((NY, TOK, 2 * HEAD_DIM), f32),
            pltpu.VMEM((NY, HEAD_DIM, 2 * HEAD_DIM), f32),
            pltpu.VMEM((NX, HEAD_DIM + 16, HEAD_DIM), bf16),
            pltpu.VMEM((NX, 8, HEAD_DIM), f32),
            pltpu.VMEM((NY, 8, HEAD_DIM), f32),
            pltpu.VMEM((8, HEAD_DIM), f32),
            pltpu.VMEM((NZ, 8, HEAD_DIM), f32),
            dma((5,)),
            dma((3,)),
            dma((NY, 3)),
            dma((3,)),
            dma((NZ,)),
            dma((NZ,)),
            dma((NX,)),
            dma((NX,)),
            dma((7,)),
            dma((7,)),
            dma((7,)),
            dma((7,)),
            dma((NX,)),
            dma((NX,)),
            dma((NX,)),
            dma((NX,)),
            dma((NY,)),
            dma((NY,)),
            dma((NZ,)),
            dma((NZ,)),
        ],
        compiler_params=pltpu.CompilerParams(collective_id=0, has_side_effects=True),
    )(
        lengths,
        positives.reshape(1, NZ),
        history,
        qkv_weight,
        norm_gain,
        pool_gain.reshape(8, HEAD_DIM),
    )
    return vec[None], loss


def solution(mesh):
    placed = (
        P("domain", "dp", "seq", None),
        P("domain", "seq", None),
        P("domain", None),
        P("domain", None),
        P("domain", "dp"),
        P(),
    )
    return jax.shard_map(
        shards,
        mesh=mesh,
        in_specs=placed,
        out_specs=(P("domain", "dp", "seq"), P("domain", "dp")),
        check_vma=False,
    )
```

```python
import jax
import jax.numpy as jnp
from jax import lax
from jax.experimental import pallas as pl
from jax.experimental.pallas import tpu as pltpu
from jax.sharding import PartitionSpec as P

HEAD_DIM = 128
NX = 4
NY = 8
NZ = 8
TOK = 256
HALF = 128
WIDTH = 1024
ROWS = 32

logit_scale = 20.0
epsilon = 1e-06
f32 = jnp.float32
bf16 = jnp.bfloat16
MESH = pl.DeviceIdType.MESH


def phi(a):
    return jnp.where(a > 0.0, a + 1.0, jnp.exp(jnp.minimum(a, 0.0)))


def tower_kernel(
    lengths_any,
    positives_any,
    hist_any,
    qkv_any,
    gain_any,
    pool_gain_any,
    vec_ref,
    loss_ref,
    lengths_ref,
    positives_ref,
    gain_ref,
    pool_gain_ref,
    tok,
    w_all,
    q_all,
    nd_all,
    st_all,
    sx,
    pall,
    vz,
    uz,
    local_sem,
    wl_sem,
    wy_send,
    wy_recv,
    wz_send,
    wz_recv,
    wx_send,
    wx_recv,
    r_send,
    r_recv,
    l_send,
    l_recv,
    s_send,
    s_recv,
    p_send,
    p_recv,
    uz_send,
    uz_recv,
):
    seq = lax.axis_index("seq")
    z = lax.axis_index("dp")
    core = lax.axis_index("domain")
    x = seq // NY
    y = lax.rem(seq, NY)

    def y_peer(k):
        return {"seq": x * NY + lax.rem(y + k, NY)}

    def x_peer(k):
        return {"seq": lax.rem(x + k, NX) * NY + y}

    def seq_peer(k):
        return {"seq": lax.rem(seq + k, NX * NY)}

    def z_peer(k):
        return {"dp": lax.rem(z + k, NZ), "domain": 1 - core}

    def w_peer(k):
        return {"dp": lax.rem(z + k, NZ)}

    def remote(src, dst, send, recv, device):
        return pltpu.make_async_remote_copy(
            src_ref=src, dst_ref=dst, send_sem=send, recv_sem=recv,
            device_id=device, device_id_type=MESH,
        )

    barrier = pltpu.get_barrier_semaphore()
    for k in range(1, NY):
        pl.semaphore_signal(barrier, inc=1, device_id=y_peer(k), device_id_type=MESH)
    for k in range(1, NX):
        pl.semaphore_signal(barrier, inc=1, device_id=x_peer(k), device_id_type=MESH)
    for k in range(NZ):
        pl.semaphore_signal(barrier, inc=1, device_id=z_peer(k), device_id_type=MESH)
    for k in range(1, NZ):
        pl.semaphore_signal(barrier, inc=1, device_id=w_peer(k), device_id_type=MESH)
    fetched = []
    for i, (src, dst) in enumerate(
        (
            (hist_any.at[0, 0], tok.at[y]),
            (lengths_any, lengths_ref),
            (positives_any, positives_ref),
            (gain_any, gain_ref),
            (pool_gain_any, pool_gain_ref),
        )
    ):
        c = pltpu.make_async_copy(src, dst, local_sem.at[i])
        c.start()
        fetched.append(c)
    pl.semaphore_wait(barrier, NY - 1 + NX - 1 + NZ + NZ - 1)
    fetched[0].wait()

    def w_slot(owner):
        return w_all.at[x, pl.ds(pl.multiple_of(owner * ROWS, ROWS), ROWS)]

    def w_part(i):
        rows = pl.ds(pl.multiple_of(z * ROWS, ROWS), ROWS)
        return w_all.at[x, rows, pl.ds(i * HEAD_DIM, HEAD_DIM)]

    def w_columns(i, head):
        start = pl.multiple_of(i * WIDTH + head * HEAD_DIM, HEAD_DIM)
        return qkv_any.at[0, :, pl.ds(start, HEAD_DIM)]

    def w_to_y(k, i):
        src = w_columns(i, lax.rem(y + k, NY))
        return remote(src, w_part(i), wy_send.at[k, i], wy_recv.at[i], y_peer(k))

    def w_own(i):
        return pltpu.make_async_copy(w_columns(i, y), w_part(i), wl_sem.at[i])

    @pl.when(y == z)
    def _():
        for i in range(3):
            w_own(i).start()
        for k in range(1, NY):
            for i in range(3):
                w_to_y(k, i).start()

    def stream(i, right, receiving):
        hop = i // 2 + (1 if receiving else 0)
        half = i % 2 if right else 1 - i % 2
        slot = lax.rem(y + (NY - hop if right else hop), NY)
        rows = pl.ds(half * HALF, HALF)
        dst = tok.at[slot, rows]
        send, recv = (r_send, r_recv) if right else (l_send, l_recv)
        return remote(dst, dst, send.at[i], recv.at[i], y_peer(1 if right else NY - 1))

    sent = []

    def send(i):
        for right in (True, False):
            c = stream(i, right, False)
            c.start()
            sent.append(c)

    def arrive(i):
        for right in (True, False):
            stream(i, right, True).wait_recv()
            if i + 2 <= 6:
                c = stream(i + 2, right, False)
                c.start()
                sent.append(c)

    send(0)
    send(1)

    @pl.when(y == z)
    def _():
        for i in range(3):
            w_own(i).wait()

    @pl.when(y != z)
    def _():
        for i in range(3):
            remote(w_part(i), w_part(i), wy_send.at[0, i], wy_recv.at[i], y_peer(1)).wait_recv()

    wz = []
    for k in range(1, NZ):
        c = remote(w_slot(z), w_slot(z), wz_send.at[k], wz_recv.at[k], w_peer(k))
        c.start()
        wz.append(c)
    for c in fetched[1:]:
        c.wait()
    length = lengths_ref[...]
    for k in range(1, NZ):
        slot = w_slot(lax.rem(z + NZ - k, NZ))
        remote(slot, slot, wz_send.at[k], wz_recv.at[k], w_peer(k)).wait_recv()
    wx = []
    for k in range(1, NX):
        c = remote(w_all.at[x], w_all.at[x], wx_send.at[k], wx_recv.at[k], x_peer(k))
        c.start()
        wx.append(c)

    gain = gain_ref[...]
    ones = jnp.ones((TOK, HEAD_DIM), bf16)
    row = lax.broadcasted_iota(jnp.int32, (TOK, 1), 0)
    causal = lax.broadcasted_iota(jnp.int32, (TOK, TOK), 0) >= lax.broadcasted_iota(
        jnp.int32, (TOK, TOK), 1
    )
    head_cols = pl.ds(pl.multiple_of(y * HEAD_DIM, HEAD_DIM), HEAD_DIM)

    def compute(src, slot, pooled):
        valid = (x * NY + slot) * TOK + row < length
        wide = src[...].astype(f32)
        scale = lax.rsqrt(jnp.sum(wide * wide, -1, keepdims=True) * (1.0 / WIDTH) + epsilon)
        normed = (wide * scale * gain).astype(bf16)
        weight = w_all[...].reshape(WIDTH, 3 * HEAD_DIM)
        proj = jnp.dot(normed, weight, preferred_element_type=f32)
        q = phi(proj[:, :HEAD_DIM]).astype(bf16)
        k = jnp.where(valid, phi(proj[:, HEAD_DIM : 2 * HEAD_DIM]), 0.0).astype(bf16)
        v1 = jnp.concatenate([proj[:, 2 * HEAD_DIM :].astype(bf16), ones], axis=1)
        scores = lax.dot_general(q, k, (((1,), (1,)), ((), ())), preferred_element_type=f32)
        low = jnp.where(causal, scores, 0.0).astype(bf16)
        q_all[slot] = q
        nd_all[slot] = jnp.dot(low, v1, preferred_element_type=f32)
        st_all[slot] = lax.dot_general(
            k, v1, (((0,), (0,)), ((), ())), preferred_element_type=f32
        )
        mine = src[:, head_cols].astype(f32)
        return pooled + jnp.sum(jnp.where(valid, mine, 0.0), axis=0, keepdims=True)

    def block(hop, pooled):
        slot = lax.rem(y + NY + hop, NY)
        return compute(tok.at[slot], slot, pooled)

    pooled = jnp.zeros((1, HEAD_DIM), f32)
    arrive(0)
    for k in range(1, NX):
        slot = w_all.at[lax.rem(x + NX - k, NX)]
        remote(slot, slot, wx_send.at[k], wx_recv.at[k], x_peer(k)).wait_recv()
    pooled = block(0, pooled)
    arrive(1)
    pooled = block(-1, pooled)
    arrive(2)
    pooled = block(1, pooled)
    arrive(3)
    pooled = block(-2, pooled)
    arrive(4)
    pooled = block(2, pooled)
    arrive(5)
    pooled = block(-3, pooled)
    pooled = block(3, pooled)
    arrive(6)
    pooled = block(4, pooled)

    total = st_all[0]
    for b in range(1, NY):
        total = total + st_all[b]
    total_rows = jnp.transpose(total[:, HEAD_DIM:])[:16]
    sx[x] = jnp.concatenate([total[:, :HEAD_DIM], total_rows], axis=0).astype(bf16)
    ss = []
    for k in range(1, NX):
        c = remote(sx.at[x], sx.at[x], s_send.at[k], s_recv.at[k], x_peer(k))
        c.start()
        ss.append(c)
    run = st_all[0]
    for b in range(1, NY):
        nd_all[b] = nd_all[b] + jnp.dot(q_all[b], run.astype(bf16), preferred_element_type=f32)
        if b + 1 < NY:
            run = run + st_all[b]
    for k in range(1, NX):
        slot = sx.at[lax.rem(x + NX - k, NX)]
        remote(slot, slot, s_send.at[k], s_recv.at[k], x_peer(k)).wait_recv()
    before = jnp.zeros((HEAD_DIM + 16, HEAD_DIM), f32)
    for g in range(NX - 1):
        before = before + jnp.where(g < x, sx[g].astype(f32), 0.0)
    total_before = jnp.broadcast_to(before[HEAD_DIM : HEAD_DIM + 1], (HEAD_DIM, HEAD_DIM))
    before = jnp.concatenate([before[:HEAD_DIM], jnp.transpose(total_before)], axis=1)
    before = before.astype(bf16)
    for b in range(NY):
        nd = nd_all[b] + jnp.dot(q_all[b], before, preferred_element_type=f32)
        valid = (x * NY + b) * TOK + row < length
        attended = nd[:, :HEAD_DIM] / nd[:, HEAD_DIM:]
        pooled = pooled + jnp.sum(jnp.where(valid, attended, 0.0), axis=0, keepdims=True)

    pall[seq] = pooled
    ps = []
    for k in range(1, NX * NY):
        c = remote(pall.at[seq], pall.at[seq], p_send.at[k], p_recv.at[k], seq_peer(k))
        c.start()
        ps.append(c)
    for k in range(1, NX * NY):
        slot = pall.at[lax.rem(seq + NX * NY - k, NX * NY)]
        remote(slot, slot, p_send.at[k], p_recv.at[k], seq_peer(k)).wait_recv()
    head_row = lax.broadcasted_iota(jnp.int32, (8, HEAD_DIM), 0)
    full = jnp.zeros((8, HEAD_DIM), f32)
    for h in range(NY):
        summed = pall[h] + pall[NY + h] + pall[2 * NY + h] + pall[3 * NY + h]
        full = jnp.where(head_row == h, summed, full)
    square = jnp.sum(jnp.sum(full * full, axis=1, keepdims=True), axis=0, keepdims=True)
    factor = lax.rsqrt(square * (1.0 / WIDTH) + epsilon)
    vec = (full * factor * pool_gain_ref[...]).astype(bf16).astype(f32)
    vz[...] = vec
    head_vec = jnp.sum(jnp.where(head_row == seq // 4, vec, 0.0), axis=0, keepdims=True)
    piece = jnp.zeros((1, ROWS), f32)
    for j in range(4):
        part = head_vec[:, j * ROWS : (j + 1) * ROWS]
        piece = jnp.where(lax.rem(seq, 4) == j, part, piece)
    vec_ref[0] = piece.astype(bf16)

    for k in range(NZ):
        c = remote(vz, uz.at[z], uz_send.at[k], uz_recv.at[k], z_peer(k))
        c.start()
        ps.append(c)
    for k in range(NZ):
        slot = uz.at[lax.rem(z + NZ - k, NZ)]
        remote(vz, slot, uz_send.at[k], uz_recv.at[k], z_peer(k)).wait_recv()
    logits = jnp.sum(jnp.sum(uz[...] * vec[None], axis=1), axis=-1, keepdims=True)
    logits = logits * (logit_scale / WIDTH)
    user = lax.broadcasted_iota(jnp.int32, (8, 1), 0)
    names = jnp.zeros((8, 1), jnp.int32)
    target = jnp.int32(0)
    for j in range(NZ):
        names = jnp.where(user == j, positives_ref[0, j], names)
        target = jnp.where(z == j, positives_ref[0, j], target)
    partner = jnp.where(core == 0, (user == target).astype(f32), (names == z).astype(f32))
    loss = jnp.log(jnp.sum(jnp.exp(logits), axis=0, keepdims=True)) - jnp.sum(
        jnp.where(partner > 0.5, logits, 0.0), axis=0, keepdims=True
    )
    loss_ref[...] = loss

    for c in wz + wx + sent + ss + ps:
        c.wait_send()

    @pl.when(y == z)
    def _():
        for k in range(1, NY):
            for i in range(3):
                w_to_y(k, i).wait_send()


def shards(history, qkv_weight, norm_gain, pool_gain, lengths, positives):
    dma = pltpu.SemaphoreType.DMA
    vmem = pl.BlockSpec(memory_space=pltpu.VMEM)
    hbm = pl.BlockSpec(memory_space=pltpu.HBM)
    vec, loss = pl.pallas_call(
        tower_kernel,
        out_shape=(
            jax.ShapeDtypeStruct((1, 1, ROWS), bf16),
            jax.ShapeDtypeStruct((1, 1), f32),
        ),
        in_specs=[hbm] * 6,
        out_specs=(vmem, vmem),
        scratch_shapes=[
            pltpu.VMEM((1, 1), jnp.int32),
            pltpu.SMEM((1, NZ), jnp.int32),
            pltpu.VMEM((1, WIDTH), f32),
            pltpu.VMEM((8, HEAD_DIM), f32),
            pltpu.VMEM((NY, TOK, WIDTH), bf16),
            pltpu.VMEM((NX, NY * ROWS, 3 * HEAD_DIM), bf16),
            pltpu.VMEM((NY, TOK, HEAD_DIM), bf16),
            pltpu.VMEM((NY, TOK, 2 * HEAD_DIM), f32),
            pltpu.VMEM((NY, HEAD_DIM, 2 * HEAD_DIM), f32),
            pltpu.VMEM((NX, HEAD_DIM + 16, HEAD_DIM), bf16),
            pltpu.VMEM((NX * NY, 1, HEAD_DIM), f32),
            pltpu.VMEM((8, HEAD_DIM), f32),
            pltpu.VMEM((NZ, 8, HEAD_DIM), f32),
            dma((5,)),
            dma((3,)),
            dma((NY, 3)),
            dma((3,)),
            dma((NZ,)),
            dma((NZ,)),
            dma((NX,)),
            dma((NX,)),
            dma((7,)),
            dma((7,)),
            dma((7,)),
            dma((7,)),
            dma((NX,)),
            dma((NX,)),
            dma((NX * NY,)),
            dma((NX * NY,)),
            dma((NZ,)),
            dma((NZ,)),
        ],
        compiler_params=pltpu.CompilerParams(collective_id=0, has_side_effects=True),
    )(
        lengths,
        positives.reshape(1, NZ),
        history,
        qkv_weight,
        norm_gain,
        pool_gain.reshape(8, HEAD_DIM),
    )
    return vec, loss


def solution(mesh):
    placed = (
        P("domain", "dp", "seq", None),
        P("domain", "seq", None),
        P("domain", None),
        P("domain", None),
        P("domain", "dp"),
        P(),
    )
    return jax.shard_map(
        shards,
        mesh=mesh,
        in_specs=placed,
        out_specs=(P("domain", "dp", "seq"), P("domain", "dp")),
        check_vma=False,
    )
```

```python
import jax
import jax.numpy as jnp
from jax import lax
from jax.experimental import pallas as pl
from jax.experimental.pallas import tpu as pltpu
from jax.sharding import PartitionSpec as P

HEAD_DIM = 128
NX = 4
NY = 8
NZ = 8
TOK = 256
HALF = 128
WIDTH = 1024
ROWS = 32

logit_scale = 20.0
epsilon = 1e-06
f32 = jnp.float32
bf16 = jnp.bfloat16
MESH = pl.DeviceIdType.MESH


def phi(a):
    return jnp.where(a > 0.0, a + 1.0, jnp.exp(jnp.minimum(a, 0.0)))


def tower_kernel(
    lengths_any,
    positives_any,
    hist_any,
    qkv_any,
    gain_any,
    pool_gain_any,
    vec_ref,
    loss_ref,
    lengths_ref,
    positives_ref,
    gain_ref,
    pool_gain_ref,
    tok,
    w_all,
    q_all,
    nd_all,
    st_all,
    sx,
    pall,
    vz,
    uz,
    ready,
    local_sem,
    wl_sem,
    wy_send,
    wy_recv,
    wz_send,
    wz_recv,
    wx_send,
    wx_recv,
    r_send,
    r_recv,
    l_send,
    l_recv,
    s_send,
    s_recv,
    p_send,
    p_recv,
    uz_send,
    uz_recv,
):
    seq = lax.axis_index("seq")
    z = lax.axis_index("dp")
    core = lax.axis_index("domain")
    x = seq // NY
    y = lax.rem(seq, NY)

    def y_peer(k):
        return {"seq": x * NY + lax.rem(y + k, NY)}

    def x_peer(k):
        return {"seq": lax.rem(x + k, NX) * NY + y}

    def seq_peer(k):
        return {"seq": lax.rem(seq + k, NX * NY)}

    def z_peer(k):
        return {"dp": lax.rem(z + k, NZ), "domain": 1 - core}

    def w_peer(k):
        return {"dp": lax.rem(z + k, NZ)}

    def remote(src, dst, send, recv, device):
        return pltpu.make_async_remote_copy(
            src_ref=src, dst_ref=dst, send_sem=send, recv_sem=recv,
            device_id=device, device_id_type=MESH,
        )

    barrier = pltpu.get_barrier_semaphore()
    for k in range(1, NY):
        pl.semaphore_signal(barrier, inc=1, device_id=y_peer(k), device_id_type=MESH)
    for k in range(1, NX):
        pl.semaphore_signal(barrier, inc=1, device_id=x_peer(k), device_id_type=MESH)
    for k in range(1, NZ):
        pl.semaphore_signal(barrier, inc=1, device_id=w_peer(k), device_id_type=MESH)
    fetched = []
    for i, (src, dst) in enumerate(
        (
            (hist_any.at[0, 0], tok.at[y]),
            (lengths_any, lengths_ref),
            (positives_any, positives_ref),
            (gain_any, gain_ref),
            (pool_gain_any, pool_gain_ref),
        )
    ):
        c = pltpu.make_async_copy(src, dst, local_sem.at[i])
        c.start()
        fetched.append(c)
    peers = NY - 1 + NX - 1 + NZ - 1

    @pl.when(core == 1)
    def _():
        pl.semaphore_wait(barrier, peers)
        pl.semaphore_signal(barrier, inc=1, device_id=z_peer(0), device_id_type=MESH)

    @pl.when(core == 0)
    def _():
        pl.semaphore_wait(barrier, peers + 1)
        pl.semaphore_signal(ready, inc=1, device_id=z_peer(0), device_id_type=MESH)

    fetched[0].wait()

    def w_slot(owner):
        return w_all.at[x, pl.ds(pl.multiple_of(owner * ROWS, ROWS), ROWS)]

    def w_part(i):
        rows = pl.ds(pl.multiple_of(z * ROWS, ROWS), ROWS)
        return w_all.at[x, rows, pl.ds(i * HEAD_DIM, HEAD_DIM)]

    def w_columns(i, head):
        start = pl.multiple_of(i * WIDTH + head * HEAD_DIM, HEAD_DIM)
        return qkv_any.at[0, :, pl.ds(start, HEAD_DIM)]

    def w_to_y(k, i):
        src = w_columns(i, lax.rem(y + k, NY))
        return remote(src, w_part(i), wy_send.at[k, i], wy_recv.at[i], y_peer(k))

    def w_own(i):
        return pltpu.make_async_copy(w_columns(i, y), w_part(i), wl_sem.at[i])

    @pl.when(y == z)
    def _():
        for i in range(3):
            w_own(i).start()
        for k in range(1, NY):
            for i in range(3):
                w_to_y(k, i).start()

    def stream(i, right, receiving):
        hop = i // 2 + (1 if receiving else 0)
        half = i % 2 if right else 1 - i % 2
        slot = lax.rem(y + (NY - hop if right else hop), NY)
        rows = pl.ds(half * HALF, HALF)
        dst = tok.at[slot, rows]
        send, recv = (r_send, r_recv) if right else (l_send, l_recv)
        return remote(dst, dst, send.at[i], recv.at[i], y_peer(1 if right else NY - 1))

    sent = []

    def send(i):
        for right in (True, False):
            c = stream(i, right, False)
            c.start()
            sent.append(c)

    def arrive(i):
        for right in (True, False):
            stream(i, right, True).wait_recv()
            if i + 2 <= 6:
                c = stream(i + 2, right, False)
                c.start()
                sent.append(c)

    send(0)
    send(1)

    @pl.when(y == z)
    def _():
        for i in range(3):
            w_own(i).wait()

    @pl.when(y != z)
    def _():
        for i in range(3):
            remote(w_part(i), w_part(i), wy_send.at[0, i], wy_recv.at[i], y_peer(1)).wait_recv()

    @pl.when(core == 1)
    def _():
        pl.semaphore_wait(ready, 1)

    wz = []
    for k in range(1, NZ):
        c = remote(w_slot(z), w_slot(z), wz_send.at[k], wz_recv.at[k], w_peer(k))
        c.start()
        wz.append(c)
    for c in fetched[1:]:
        c.wait()
    length = lengths_ref[...]
    arrive(0)
    for k in range(1, NZ):
        slot = w_slot(lax.rem(z + NZ - k, NZ))
        remote(slot, slot, wz_send.at[k], wz_recv.at[k], w_peer(k)).wait_recv()
    wx = []
    for k in range(1, NX):
        c = remote(w_all.at[x], w_all.at[x], wx_send.at[k], wx_recv.at[k], x_peer(k))
        c.start()
        wx.append(c)

    gain = gain_ref[...]
    ones = jnp.ones((TOK, HEAD_DIM), bf16)
    row = lax.broadcasted_iota(jnp.int32, (TOK, 1), 0)
    causal = lax.broadcasted_iota(jnp.int32, (TOK, TOK), 0) >= lax.broadcasted_iota(
        jnp.int32, (TOK, TOK), 1
    )
    head_cols = pl.ds(pl.multiple_of(y * HEAD_DIM, HEAD_DIM), HEAD_DIM)

    def compute(src, slot, pooled):
        valid = (x * NY + slot) * TOK + row < length
        wide = src[...].astype(f32)
        scale = lax.rsqrt(jnp.sum(wide * wide, -1, keepdims=True) * (1.0 / WIDTH) + epsilon)
        normed = (wide * scale * gain).astype(bf16)
        weight = w_all[...].reshape(WIDTH, 3 * HEAD_DIM)
        proj = jnp.dot(normed, weight, preferred_element_type=f32)
        q = phi(proj[:, :HEAD_DIM]).astype(bf16)
        k = jnp.where(valid, phi(proj[:, HEAD_DIM : 2 * HEAD_DIM]), 0.0).astype(bf16)
        v1 = jnp.concatenate([proj[:, 2 * HEAD_DIM :].astype(bf16), ones], axis=1)
        scores = lax.dot_general(q, k, (((1,), (1,)), ((), ())), preferred_element_type=f32)
        low = jnp.where(causal, scores, 0.0).astype(bf16)
        q_all[slot] = q
        nd_all[slot] = jnp.dot(low, v1, preferred_element_type=f32)
        st_all[slot] = lax.dot_general(
            k, v1, (((0,), (0,)), ((), ())), preferred_element_type=f32
        )
        mine = src[:, head_cols].astype(f32)
        return pooled + jnp.sum(jnp.where(valid, mine, 0.0), axis=0, keepdims=True)

    def block(hop, pooled):
        slot = lax.rem(y + NY + hop, NY)
        return compute(tok.at[slot], slot, pooled)

    pooled = jnp.zeros((1, HEAD_DIM), f32)
    arrive(1)
    arrive(2)
    for k in range(1, NX):
        slot = w_all.at[lax.rem(x + NX - k, NX)]
        remote(slot, slot, wx_send.at[k], wx_recv.at[k], x_peer(k)).wait_recv()
    pooled = block(0, pooled)
    arrive(3)
    pooled = block(-1, pooled)
    pooled = block(1, pooled)
    arrive(4)
    pooled = block(-2, pooled)
    pooled = block(2, pooled)
    arrive(5)
    pooled = block(-3, pooled)
    pooled = block(3, pooled)
    arrive(6)
    pooled = block(4, pooled)

    total = st_all[0]
    for b in range(1, NY):
        total = total + st_all[b]
    total_rows = jnp.transpose(total[:, HEAD_DIM:])[:16]
    sx[x] = jnp.concatenate([total[:, :HEAD_DIM], total_rows], axis=0).astype(bf16)
    ss = []
    for k in range(1, NX):
        c = remote(sx.at[x], sx.at[x], s_send.at[k], s_recv.at[k], x_peer(k))
        c.start()
        ss.append(c)
    run = st_all[0]
    for b in range(1, NY):
        nd_all[b] = nd_all[b] + jnp.dot(q_all[b], run.astype(bf16), preferred_element_type=f32)
        if b + 1 < NY:
            run = run + st_all[b]
    for k in range(1, NX):
        slot = sx.at[lax.rem(x + NX - k, NX)]
        remote(slot, slot, s_send.at[k], s_recv.at[k], x_peer(k)).wait_recv()
    before = jnp.zeros((HEAD_DIM + 16, HEAD_DIM), f32)
    for g in range(NX - 1):
        before = before + jnp.where(g < x, sx[g].astype(f32), 0.0)
    total_before = jnp.broadcast_to(before[HEAD_DIM : HEAD_DIM + 1], (HEAD_DIM, HEAD_DIM))
    before = jnp.concatenate([before[:HEAD_DIM], jnp.transpose(total_before)], axis=1)
    before = before.astype(bf16)
    for b in range(NY):
        nd = nd_all[b] + jnp.dot(q_all[b], before, preferred_element_type=f32)
        valid = (x * NY + b) * TOK + row < length
        attended = nd[:, :HEAD_DIM] / nd[:, HEAD_DIM:]
        pooled = pooled + jnp.sum(jnp.where(valid, attended, 0.0), axis=0, keepdims=True)

    pall[seq] = pooled
    ps = []
    for k in range(1, NX * NY):
        c = remote(pall.at[seq], pall.at[seq], p_send.at[k], p_recv.at[k], seq_peer(k))
        c.start()
        ps.append(c)
    for k in range(1, NX * NY):
        slot = pall.at[lax.rem(seq + NX * NY - k, NX * NY)]
        remote(slot, slot, p_send.at[k], p_recv.at[k], seq_peer(k)).wait_recv()
    head_row = lax.broadcasted_iota(jnp.int32, (8, HEAD_DIM), 0)
    full = jnp.zeros((8, HEAD_DIM), f32)
    for h in range(NY):
        summed = pall[h] + pall[NY + h] + pall[2 * NY + h] + pall[3 * NY + h]
        full = jnp.where(head_row == h, summed, full)
    square = jnp.sum(jnp.sum(full * full, axis=1, keepdims=True), axis=0, keepdims=True)
    factor = lax.rsqrt(square * (1.0 / WIDTH) + epsilon)
    vec = (full * factor * pool_gain_ref[...]).astype(bf16).astype(f32)
    vz[...] = vec
    head_vec = jnp.sum(jnp.where(head_row == seq // 4, vec, 0.0), axis=0, keepdims=True)
    piece = jnp.zeros((1, ROWS), f32)
    for j in range(4):
        part = head_vec[:, j * ROWS : (j + 1) * ROWS]
        piece = jnp.where(lax.rem(seq, 4) == j, part, piece)
    vec_ref[0] = piece.astype(bf16)

    for k in range(NZ):
        c = remote(vz, uz.at[z], uz_send.at[k], uz_recv.at[k], z_peer(k))
        c.start()
        ps.append(c)
    for k in range(NZ):
        slot = uz.at[lax.rem(z + NZ - k, NZ)]
        remote(vz, slot, uz_send.at[k], uz_recv.at[k], z_peer(k)).wait_recv()
    logits = jnp.sum(jnp.sum(uz[...] * vec[None], axis=1), axis=-1, keepdims=True)
    logits = logits * (logit_scale / WIDTH)
    user = lax.broadcasted_iota(jnp.int32, (8, 1), 0)
    names = jnp.zeros((8, 1), jnp.int32)
    target = jnp.int32(0)
    for j in range(NZ):
        names = jnp.where(user == j, positives_ref[0, j], names)
        target = jnp.where(z == j, positives_ref[0, j], target)
    partner = jnp.where(core == 0, (user == target).astype(f32), (names == z).astype(f32))
    loss = jnp.log(jnp.sum(jnp.exp(logits), axis=0, keepdims=True)) - jnp.sum(
        jnp.where(partner > 0.5, logits, 0.0), axis=0, keepdims=True
    )
    loss_ref[...] = loss

    for c in wz + wx + sent + ss + ps:
        c.wait_send()

    @pl.when(y == z)
    def _():
        for k in range(1, NY):
            for i in range(3):
                w_to_y(k, i).wait_send()


def shards(history, qkv_weight, norm_gain, pool_gain, lengths, positives):
    dma = pltpu.SemaphoreType.DMA
    vmem = pl.BlockSpec(memory_space=pltpu.VMEM)
    hbm = pl.BlockSpec(memory_space=pltpu.HBM)
    vec, loss = pl.pallas_call(
        tower_kernel,
        out_shape=(
            jax.ShapeDtypeStruct((1, 1, ROWS), bf16),
            jax.ShapeDtypeStruct((1, 1), f32),
        ),
        in_specs=[hbm] * 6,
        out_specs=(vmem, vmem),
        scratch_shapes=[
            pltpu.VMEM((1, 1), jnp.int32),
            pltpu.SMEM((1, NZ), jnp.int32),
            pltpu.VMEM((1, WIDTH), f32),
            pltpu.VMEM((8, HEAD_DIM), f32),
            pltpu.VMEM((NY, TOK, WIDTH), bf16),
            pltpu.VMEM((NX, NY * ROWS, 3 * HEAD_DIM), bf16),
            pltpu.VMEM((NY, TOK, HEAD_DIM), bf16),
            pltpu.VMEM((NY, TOK, 2 * HEAD_DIM), f32),
            pltpu.VMEM((NY, HEAD_DIM, 2 * HEAD_DIM), f32),
            pltpu.VMEM((NX, HEAD_DIM + 16, HEAD_DIM), bf16),
            pltpu.VMEM((NX * NY, 1, HEAD_DIM), f32),
            pltpu.VMEM((8, HEAD_DIM), f32),
            pltpu.VMEM((NZ, 8, HEAD_DIM), f32),
            pltpu.SemaphoreType.REGULAR,
            dma((5,)),
            dma((3,)),
            dma((NY, 3)),
            dma((3,)),
            dma((NZ,)),
            dma((NZ,)),
            dma((NX,)),
            dma((NX,)),
            dma((7,)),
            dma((7,)),
            dma((7,)),
            dma((7,)),
            dma((NX,)),
            dma((NX,)),
            dma((NX * NY,)),
            dma((NX * NY,)),
            dma((NZ,)),
            dma((NZ,)),
        ],
        compiler_params=pltpu.CompilerParams(collective_id=0, has_side_effects=True),
    )(
        lengths,
        positives.reshape(1, NZ),
        history,
        qkv_weight,
        norm_gain,
        pool_gain.reshape(8, HEAD_DIM),
    )
    return vec, loss


def solution(mesh):
    placed = (
        P("domain", "dp", "seq", None),
        P("domain", "seq", None),
        P("domain", None),
        P("domain", None),
        P("domain", "dp"),
        P(),
    )
    return jax.shard_map(
        shards,
        mesh=mesh,
        in_specs=placed,
        out_specs=(P("domain", "dp", "seq"), P("domain", "dp")),
        check_vma=False,
    )
```

```python
import jax
import jax.numpy as jnp
from jax import lax
from jax.experimental import pallas as pl
from jax.experimental.pallas import tpu as pltpu
from jax.sharding import PartitionSpec as P

HEAD_DIM = 128
NX = 4
NY = 8
NZ = 8
TOK = 256
HALF = 128
WIDTH = 1024
ROWS = 32

logit_scale = 20.0
epsilon = 1e-06
f32 = jnp.float32
bf16 = jnp.bfloat16
MESH = pl.DeviceIdType.MESH


def phi(a):
    return jnp.where(a > 0.0, a + 1.0, jnp.exp(jnp.minimum(a, 0.0)))


def tower_kernel(
    lengths_any,
    positives_any,
    hist_any,
    qkv_any,
    gain_any,
    pool_gain_any,
    vec_ref,
    loss_ref,
    lengths_ref,
    positives_ref,
    gain_ref,
    pool_gain_ref,
    tok,
    w_all,
    q_all,
    nd_all,
    st_all,
    sx,
    pall,
    vz,
    uz,
    ready,
    local_sem,
    wl_sem,
    wy_send,
    wy_recv,
    wz_send,
    wz_recv,
    wx_send,
    wx_recv,
    r_send,
    r_recv,
    l_send,
    l_recv,
    s_send,
    s_recv,
    p_send,
    p_recv,
    uz_send,
    uz_recv,
):
    seq = lax.axis_index("seq")
    z = lax.axis_index("dp")
    core = lax.axis_index("domain")
    x = seq // NY
    y = lax.rem(seq, NY)

    def y_peer(k):
        return {"seq": x * NY + lax.rem(y + k, NY)}

    def x_peer(k):
        return {"seq": lax.rem(x + k, NX) * NY + y}

    def seq_peer(k):
        return {"seq": lax.rem(seq + k, NX * NY)}

    def z_peer(k):
        return {"dp": lax.rem(z + k, NZ), "domain": 1 - core}

    def w_peer(k):
        return {"dp": lax.rem(z + k, NZ)}

    def remote(src, dst, send, recv, device):
        return pltpu.make_async_remote_copy(
            src_ref=src, dst_ref=dst, send_sem=send, recv_sem=recv,
            device_id=device, device_id_type=MESH,
        )

    barrier = pltpu.get_barrier_semaphore()
    for k in range(1, NY):
        pl.semaphore_signal(barrier, inc=1, device_id=y_peer(k), device_id_type=MESH)
    for k in range(1, NX):
        pl.semaphore_signal(barrier, inc=1, device_id=x_peer(k), device_id_type=MESH)
    for k in range(1, NZ):
        pl.semaphore_signal(barrier, inc=1, device_id=w_peer(k), device_id_type=MESH)
    fetched = []
    for i, (src, dst) in enumerate(
        (
            (hist_any.at[0, 0], tok.at[y]),
            (lengths_any, lengths_ref),
            (positives_any, positives_ref),
            (gain_any, gain_ref),
            (pool_gain_any, pool_gain_ref),
        )
    ):
        c = pltpu.make_async_copy(src, dst, local_sem.at[i])
        c.start()
        fetched.append(c)
    peers = NY - 1 + NX - 1 + NZ - 1

    @pl.when(core == 1)
    def _():
        pl.semaphore_wait(barrier, peers)
        pl.semaphore_signal(barrier, inc=1, device_id=z_peer(0), device_id_type=MESH)

    @pl.when(core == 0)
    def _():
        pl.semaphore_wait(barrier, peers + 1)
        pl.semaphore_signal(ready, inc=1, device_id=z_peer(0), device_id_type=MESH)

    fetched[0].wait()

    def w_slot(owner):
        return w_all.at[x, pl.ds(pl.multiple_of(owner * ROWS, ROWS), ROWS)]

    def w_part(i):
        rows = pl.ds(pl.multiple_of(z * ROWS, ROWS), ROWS)
        return w_all.at[x, rows, pl.ds(i * HEAD_DIM, HEAD_DIM)]

    def w_columns(i, head):
        start = pl.multiple_of(i * WIDTH + head * HEAD_DIM, HEAD_DIM)
        return qkv_any.at[0, :, pl.ds(start, HEAD_DIM)]

    def w_to_y(k, i):
        src = w_columns(i, lax.rem(y + k, NY))
        return remote(src, w_part(i), wy_send.at[k, i], wy_recv.at[i], y_peer(k))

    def w_own(i):
        return pltpu.make_async_copy(w_columns(i, y), w_part(i), wl_sem.at[i])

    def stream(i, right, receiving):
        hop = i // 2 + (1 if receiving else 0)
        half = i % 2 if right else 1 - i % 2
        slot = lax.rem(y + (NY - hop if right else hop), NY)
        rows = pl.ds(half * HALF, HALF)
        dst = tok.at[slot, rows]
        send, recv = (r_send, r_recv) if right else (l_send, l_recv)
        return remote(dst, dst, send.at[i], recv.at[i], y_peer(1 if right else NY - 1))

    sent = []

    def send(i):
        for right in (True, False):
            c = stream(i, right, False)
            c.start()
            sent.append(c)

    def arrive(i):
        for right in (True, False):
            stream(i, right, True).wait_recv()
            if i + 2 <= 6:
                c = stream(i + 2, right, False)
                c.start()
                sent.append(c)

    send(0)
    @pl.when(y == z)
    def _():
        for i in range(3):
            w_own(i).start()
        for k in range(1, NY):
            for i in range(3):
                w_to_y(k, i).start()

    send(1)

    @pl.when(y == z)
    def _():
        for i in range(3):
            w_own(i).wait()

    @pl.when(y != z)
    def _():
        for i in range(3):
            remote(w_part(i), w_part(i), wy_send.at[0, i], wy_recv.at[i], y_peer(1)).wait_recv()

    @pl.when(core == 1)
    def _():
        pl.semaphore_wait(ready, 1)

    wz = []
    for k in range(1, NZ):
        c = remote(w_slot(z), w_slot(z), wz_send.at[k], wz_recv.at[k], w_peer(k))
        c.start()
        wz.append(c)
    for c in fetched[1:]:
        c.wait()
    length = lengths_ref[...]
    arrive(0)
    for k in range(1, NZ):
        slot = w_slot(lax.rem(z + NZ - k, NZ))
        remote(slot, slot, wz_send.at[k], wz_recv.at[k], w_peer(k)).wait_recv()
    wx = []
    for k in range(1, NX):
        c = remote(w_all.at[x], w_all.at[x], wx_send.at[k], wx_recv.at[k], x_peer(k))
        c.start()
        wx.append(c)

    gain = gain_ref[...]
    ones = jnp.ones((TOK, HEAD_DIM), bf16)
    row = lax.broadcasted_iota(jnp.int32, (TOK, 1), 0)
    causal = lax.broadcasted_iota(jnp.int32, (TOK, TOK), 0) >= lax.broadcasted_iota(
        jnp.int32, (TOK, TOK), 1
    )
    head_cols = pl.ds(pl.multiple_of(y * HEAD_DIM, HEAD_DIM), HEAD_DIM)

    def keys(slot):
        src = tok.at[slot]
        valid = (x * NY + slot) * TOK + row < length
        wide = src[...].astype(f32)
        scale = lax.rsqrt(jnp.sum(wide * wide, -1, keepdims=True) * (1.0 / WIDTH) + epsilon)
        normed = (wide * scale * gain).astype(bf16)
        weight = w_all[...].reshape(WIDTH, 3 * HEAD_DIM)
        proj = jnp.dot(normed, weight, preferred_element_type=f32)
        k = jnp.where(valid, phi(proj[:, HEAD_DIM : 2 * HEAD_DIM]), 0.0).astype(bf16)
        v1 = jnp.concatenate([proj[:, 2 * HEAD_DIM :].astype(bf16), ones], axis=1)
        st_all[slot] = lax.dot_general(
            k, v1, (((0,), (0,)), ((), ())), preferred_element_type=f32
        )
        return proj[:, :HEAD_DIM], k, v1, valid

    def attend(slot, found, pooled):
        query_raw, k, v1, valid = found
        q = phi(query_raw).astype(bf16)
        scores = lax.dot_general(q, k, (((1,), (1,)), ((), ())), preferred_element_type=f32)
        low = jnp.where(causal, scores, 0.0).astype(bf16)
        q_all[slot] = q
        nd_all[slot] = jnp.dot(low, v1, preferred_element_type=f32)
        mine = tok.at[slot][:, head_cols].astype(f32)
        return pooled + jnp.sum(jnp.where(valid, mine, 0.0), axis=0, keepdims=True)

    def block(hop, pooled):
        slot = lax.rem(y + NY + hop, NY)
        return attend(slot, keys(slot), pooled)

    pooled = jnp.zeros((1, HEAD_DIM), f32)
    arrive(1)
    arrive(2)
    for k in range(1, NX):
        slot = w_all.at[lax.rem(x + NX - k, NX)]
        remote(slot, slot, wx_send.at[k], wx_recv.at[k], x_peer(k)).wait_recv()
    pooled = block(0, pooled)
    arrive(3)
    pooled = block(-1, pooled)
    pooled = block(1, pooled)
    arrive(4)
    pooled = block(-2, pooled)
    pooled = block(2, pooled)
    arrive(5)
    pooled = block(-3, pooled)
    pooled = block(3, pooled)
    arrive(6)
    last = lax.rem(y + NY // 2, NY)
    found = keys(last)

    total = st_all[0]
    for b in range(1, NY):
        total = total + st_all[b]
    total_rows = jnp.transpose(total[:, HEAD_DIM:])[:16]
    sx[x] = jnp.concatenate([total[:, :HEAD_DIM], total_rows], axis=0).astype(bf16)
    ss = []
    for k in range(1, NX):
        c = remote(sx.at[x], sx.at[x], s_send.at[k], s_recv.at[k], x_peer(k))
        c.start()
        ss.append(c)
    pooled = attend(last, found, pooled)
    run = st_all[0]
    for b in range(1, NY):
        nd_all[b] = nd_all[b] + jnp.dot(q_all[b], run.astype(bf16), preferred_element_type=f32)
        if b + 1 < NY:
            run = run + st_all[b]
    for k in range(1, NX):
        slot = sx.at[lax.rem(x + NX - k, NX)]
        remote(slot, slot, s_send.at[k], s_recv.at[k], x_peer(k)).wait_recv()
    before = jnp.zeros((HEAD_DIM + 16, HEAD_DIM), f32)
    for g in range(NX - 1):
        before = before + jnp.where(g < x, sx[g].astype(f32), 0.0)
    total_before = jnp.broadcast_to(before[HEAD_DIM : HEAD_DIM + 1], (HEAD_DIM, HEAD_DIM))
    before = jnp.concatenate([before[:HEAD_DIM], jnp.transpose(total_before)], axis=1)
    before = before.astype(bf16)
    for b in range(NY):
        nd = nd_all[b] + jnp.dot(q_all[b], before, preferred_element_type=f32)
        valid = (x * NY + b) * TOK + row < length
        attended = nd[:, :HEAD_DIM] / nd[:, HEAD_DIM:]
        pooled = pooled + jnp.sum(jnp.where(valid, attended, 0.0), axis=0, keepdims=True)

    pall[seq] = pooled
    ps = []
    for k in range(1, NX * NY):
        c = remote(pall.at[seq], pall.at[seq], p_send.at[k], p_recv.at[k], seq_peer(k))
        c.start()
        ps.append(c)
    for k in range(1, NX * NY):
        slot = pall.at[lax.rem(seq + NX * NY - k, NX * NY)]
        remote(slot, slot, p_send.at[k], p_recv.at[k], seq_peer(k)).wait_recv()
    head_row = lax.broadcasted_iota(jnp.int32, (8, HEAD_DIM), 0)
    full = jnp.zeros((8, HEAD_DIM), f32)
    for h in range(NY):
        summed = pall[h] + pall[NY + h] + pall[2 * NY + h] + pall[3 * NY + h]
        full = jnp.where(head_row == h, summed, full)
    square = jnp.sum(jnp.sum(full * full, axis=1, keepdims=True), axis=0, keepdims=True)
    factor = lax.rsqrt(square * (1.0 / WIDTH) + epsilon)
    vec = (full * factor * pool_gain_ref[...]).astype(bf16).astype(f32)
    vz[...] = vec
    head_vec = jnp.sum(jnp.where(head_row == seq // 4, vec, 0.0), axis=0, keepdims=True)
    piece = jnp.zeros((1, ROWS), f32)
    for j in range(4):
        part = head_vec[:, j * ROWS : (j + 1) * ROWS]
        piece = jnp.where(lax.rem(seq, 4) == j, part, piece)
    vec_ref[0] = piece.astype(bf16)

    for k in range(NZ):
        c = remote(vz, uz.at[z], uz_send.at[k], uz_recv.at[k], z_peer(k))
        c.start()
        ps.append(c)
    for k in range(NZ):
        slot = uz.at[lax.rem(z + NZ - k, NZ)]
        remote(vz, slot, uz_send.at[k], uz_recv.at[k], z_peer(k)).wait_recv()
    logits = jnp.sum(jnp.sum(uz[...] * vec[None], axis=1), axis=-1, keepdims=True)
    logits = logits * (logit_scale / WIDTH)
    user = lax.broadcasted_iota(jnp.int32, (8, 1), 0)
    names = jnp.zeros((8, 1), jnp.int32)
    target = jnp.int32(0)
    for j in range(NZ):
        names = jnp.where(user == j, positives_ref[0, j], names)
        target = jnp.where(z == j, positives_ref[0, j], target)
    partner = jnp.where(core == 0, (user == target).astype(f32), (names == z).astype(f32))
    loss = jnp.log(jnp.sum(jnp.exp(logits), axis=0, keepdims=True)) - jnp.sum(
        jnp.where(partner > 0.5, logits, 0.0), axis=0, keepdims=True
    )
    loss_ref[...] = loss

    for c in wz + wx + sent + ss + ps:
        c.wait_send()

    @pl.when(y == z)
    def _():
        for k in range(1, NY):
            for i in range(3):
                w_to_y(k, i).wait_send()


def shards(history, qkv_weight, norm_gain, pool_gain, lengths, positives):
    dma = pltpu.SemaphoreType.DMA
    vmem = pl.BlockSpec(memory_space=pltpu.VMEM)
    hbm = pl.BlockSpec(memory_space=pltpu.HBM)
    vec, loss = pl.pallas_call(
        tower_kernel,
        out_shape=(
            jax.ShapeDtypeStruct((1, 1, ROWS), bf16),
            jax.ShapeDtypeStruct((1, 1), f32),
        ),
        in_specs=[hbm] * 6,
        out_specs=(vmem, vmem),
        scratch_shapes=[
            pltpu.VMEM((1, 1), jnp.int32),
            pltpu.SMEM((1, NZ), jnp.int32),
            pltpu.VMEM((1, WIDTH), f32),
            pltpu.VMEM((8, HEAD_DIM), f32),
            pltpu.VMEM((NY, TOK, WIDTH), bf16),
            pltpu.VMEM((NX, NY * ROWS, 3 * HEAD_DIM), bf16),
            pltpu.VMEM((NY, TOK, HEAD_DIM), bf16),
            pltpu.VMEM((NY, TOK, 2 * HEAD_DIM), f32),
            pltpu.VMEM((NY, HEAD_DIM, 2 * HEAD_DIM), f32),
            pltpu.VMEM((NX, HEAD_DIM + 16, HEAD_DIM), bf16),
            pltpu.VMEM((NX * NY, 1, HEAD_DIM), f32),
            pltpu.VMEM((8, HEAD_DIM), f32),
            pltpu.VMEM((NZ, 8, HEAD_DIM), f32),
            pltpu.SemaphoreType.REGULAR,
            dma((5,)),
            dma((3,)),
            dma((NY, 3)),
            dma((3,)),
            dma((NZ,)),
            dma((NZ,)),
            dma((NX,)),
            dma((NX,)),
            dma((7,)),
            dma((7,)),
            dma((7,)),
            dma((7,)),
            dma((NX,)),
            dma((NX,)),
            dma((NX * NY,)),
            dma((NX * NY,)),
            dma((NZ,)),
            dma((NZ,)),
        ],
        compiler_params=pltpu.CompilerParams(collective_id=0, has_side_effects=True),
    )(
        lengths,
        positives.reshape(1, NZ),
        history,
        qkv_weight,
        norm_gain,
        pool_gain.reshape(8, HEAD_DIM),
    )
    return vec, loss


def solution(mesh):
    placed = (
        P("domain", "dp", "seq", None),
        P("domain", "seq", None),
        P("domain", None),
        P("domain", None),
        P("domain", "dp"),
        P(),
    )
    return jax.shard_map(
        shards,
        mesh=mesh,
        in_specs=placed,
        out_specs=(P("domain", "dp", "seq"), P("domain", "dp")),
        check_vma=False,
    )
```
